256 devices in a mesh: section: 8 (over z), dp: 32 (over x, y, core).
Axes of the slice: x: 4, y: 4, z: 8, core: 2. Of those that a mesh axis runs over, the one named last changes fastest.
Arguments:
- output_gradient: bfloat16 [8, 4096, 2048], P('section', 'dp'), may hold values from -6 to 6
- saved_input: bfloat16 [8, 4096, 8192], P('section', 'dp'), may hold values from -6 to 6
- frozen_matrix: bfloat16 [8, 8192, 2048], P('section', 'dp'), may hold values from -0.0625 to 0.0625
- adapter_down_maps: bfloat16 [8, 8192, 2048], P('section', None, 'dp'), may hold values from -0.0625 to 0.0625
- adapter_up_maps: bfloat16 [8, 2048, 2048], P('section', None, 'dp'), may hold values from -0.125 to 0.125
- token_tenants: int32 [8, 4096], P('section'), may hold values from 0 to 31, never falling along the last dimension, each value on 1 to 256 neighbouring positions
- tenant_slot_lookup: int32 [8, 32], P('section'), may hold values from 0 to 31, each once within a row
Outputs:
- passed_grad: bfloat16 [8, 4096, 8192], P('section', 'dp')
- down_gradient: bfloat16 [8, 8192, 2048], P('section', None, 'dp')
- up_gradient: bfloat16 [8, 2048, 2048], P('section', None, 'dp')
The draws below stay inside these ranges and needn't reach their ends.
Inputs may be any that keep to these rules, and one draw needn't show every extreme that they name: `token_tenants`: within a section the ids never fall; each of the 32 tenants has 1 to 256 tokens, one exactly 256. `tenant_slot_lookup`: each section's row is a permutation.
All inputs are finite; a program needn't handle non-finite values.
Results may differ from the reference program's by a relative error of at most 0.005.
Values may be sent and summed in bfloat16 or wider, within the bound.
A program may use at most 128 MiB of HBM per device.

```python
import math
import jax
import jax.numpy as jnp
import numpy as np

MODEL_WIDTH = 8192
KEY_VALUE_WIDTH = 2048
ADAPTER_RANK = 64
RELAY_SECTIONS = 8
TOKENS = 4096
TENANT_COUNT = 32
MOST = 256


def block_levels(stream_key, extent, pieces, low, largest):
    factor_of, own = 1.0, jax.random.fold_in(stream_key, 6)
    for position, blocks in pieces:
        draws = jnp.exp(jax.random.uniform(jax.random.fold_in(own, position), (blocks,), jnp.float32, low / len(pieces), largest / len(pieces)))
        factor_of = factor_of * jnp.repeat(draws, extent[position] // blocks).reshape([-1 if axis == position else 1 for axis in range(len(extent))])
    return factor_of


def profile(number_of, total, reach, slope):
    loads = [(1 << 20) // math.isqrt(grade ** slope) + 1 for grade in range(2, number_of + 1)]
    rest, holding = total - reach - (number_of - 1), [1] * (number_of - 1)
    while rest > 0:
        free = [i for i in range(number_of - 1) if holding[i] < reach]
        mass, left = sum([loads[i] for i in free]), rest
        for i in free:
            addition = min(reach - holding[i], max(1, left * loads[i] // mass), rest)
            holding[i] = holding[i] + addition
            rest = rest - addition
    return np.array([reach] + holding)


def uneven(stream_key, number_of, total, limit, skew):
    if number_of == 2:
        one = jax.random.randint(stream_key, (), max(1, total - limit), min(limit, total - 1) + 1)
        return jnp.stack([one, total - one])
    sizes = jnp.asarray(profile(number_of, total, limit, skew), jnp.int32)
    couples = (number_of - 1) // 2
    giver, taker = sizes[1:1 + 2 * couples:2], sizes[2:2 + 2 * couples:2]
    slack = jnp.minimum(giver - 1, limit - taker)
    shifted = jax.random.randint(jax.random.fold_in(stream_key, 1), (couples,), 0, 1 << 20) % (slack + 1)
    sizes = sizes.at[1:1 + 2 * couples:2].set(giver - shifted).at[2:2 + 2 * couples:2].set(taker + shifted)
    return sizes[jax.random.permutation(jax.random.fold_in(stream_key, 2), number_of)]


def noise(own_key, shape, deviation, bound, pieces=(), held_as=jnp.bfloat16):
    gain = block_levels(own_key, shape, pieces, -0.22, 0.18) if pieces else 1.0
    array = jax.random.normal(own_key, shape, jnp.float32) * deviation * gain
    return jnp.minimum(jnp.maximum(array, -bound), bound).astype(held_as)


def setup_inputs(seed: int = 0) -> dict:
    splits = jax.random.split(jax.random.key(seed), 8)
    return {
        "output_gradient": noise(splits[0], (RELAY_SECTIONS, TOKENS, KEY_VALUE_WIDTH), 1.0, 6.0, ((0, 8), (1, 32))),
        "saved_input": noise(splits[1], (RELAY_SECTIONS, TOKENS, MODEL_WIDTH), 1.0, 6.0, ((0, 8), (1, 32))),
        "frozen_matrix": noise(splits[2], (RELAY_SECTIONS, MODEL_WIDTH, KEY_VALUE_WIDTH), MODEL_WIDTH ** -0.5, 0.0625, ((0, 8), (1, 32))),
        "adapter_down_maps": noise(splits[3], (RELAY_SECTIONS, MODEL_WIDTH, TENANT_COUNT * ADAPTER_RANK), MODEL_WIDTH ** -0.5, 0.0625, ((0, 8), (2, 32))),
        "adapter_up_maps": noise(splits[4], (RELAY_SECTIONS, KEY_VALUE_WIDTH, TENANT_COUNT * ADAPTER_RANK), KEY_VALUE_WIDTH ** -0.5, 0.125, ((0, 8), (2, 32))),
        "token_tenants": jax.vmap(lambda own: jnp.searchsorted(jnp.cumsum(uneven(own, TENANT_COUNT, TOKENS, MOST, 2)), jnp.arange(TOKENS), side="right"))(jax.random.split(splits[5], RELAY_SECTIONS)).reshape((RELAY_SECTIONS, TOKENS)).astype(jnp.int32),
        "tenant_slot_lookup": jax.vmap(lambda own: jax.random.permutation(own, TENANT_COUNT))(jax.random.split(splits[6], RELAY_SECTIONS)).reshape((RELAY_SECTIONS, TENANT_COUNT)).astype(jnp.int32),
    }


adapter_scale = 2.0


def block_layout(tenant_row, slot_table, tenants, most):
    tokens = tenant_row.shape[0]
    tenant_range = jnp.arange(tenants, dtype=jnp.int32)
    member = (tenant_range[:, None] == tenant_row[None, :]).astype(jnp.int32)
    counts = jnp.sum(member, axis=1).astype(jnp.int32)
    starts = (jnp.cumsum(counts).astype(jnp.int32) - counts).astype(jnp.int32)
    owner_match = (slot_table[None, :] == tenant_range[:, None]).astype(jnp.int32)
    slot_start = jnp.sum(owner_match * starts[None, :], axis=1).astype(jnp.int32)
    slot_count = jnp.sum(owner_match * counts[None, :], axis=1).astype(jnp.int32)
    place = jnp.arange(most, dtype=jnp.int32)
    live_slot = place[None, :] < slot_count[:, None]
    row_index = jnp.minimum(slot_start[:, None] + place[None, :], tokens - 1).astype(jnp.int32)
    token_slot = jnp.sum(member * slot_table[:, None], axis=0).astype(jnp.int32)
    token_start = jnp.sum(member * starts[:, None], axis=0).astype(jnp.int32)
    token_place = (token_slot * most + jnp.arange(tokens, dtype=jnp.int32) - token_start).astype(jnp.int32)
    return row_index, live_slot, token_place


def masked_rows(rows, row_index, live_slot):
    picked = rows[row_index]
    return jnp.where(live_slot[:, :, None], picked, jnp.zeros((), picked.dtype))


def section_gradients(grad_rows, saved_rows, weight, down_maps, up_maps, tenant_row, slot_table):
    row_index, live_slot, token_place = block_layout(tenant_row, slot_table, TENANT_COUNT, MOST)
    gradient_blocks = masked_rows(grad_rows, row_index, live_slot).astype(jnp.float32)
    saved_input_blocks = masked_rows(saved_rows, row_index, live_slot).astype(jnp.float32)
    down_three = down_maps.reshape(MODEL_WIDTH, TENANT_COUNT, ADAPTER_RANK).astype(jnp.float32)
    up_three = up_maps.reshape(KEY_VALUE_WIDTH, TENANT_COUNT, ADAPTER_RANK).astype(jnp.float32)
    rank_up_values = jnp.einsum("kpe,ekr->kpr", gradient_blocks, up_three).astype(jnp.bfloat16)
    rank_down_values = jnp.einsum("kpd,dkr->kpr", saved_input_blocks, down_three).astype(jnp.bfloat16)
    adapter_blocks = jnp.einsum("kpr,dkr->kpd", rank_up_values.astype(jnp.float32), down_three)
    adapter_slot = adapter_blocks.reshape(TENANT_COUNT * MOST, MODEL_WIDTH)[token_place]
    frozen_product = jnp.dot(grad_rows, weight.T, preferred_element_type=jnp.float32)
    input_gradient = (frozen_product + adapter_scale * adapter_slot).astype(jnp.bfloat16)
    down_gradient = (adapter_scale * jnp.einsum("tfv,tfy->vty", saved_input_blocks, rank_up_values.astype(jnp.float32))).reshape(MODEL_WIDTH, TENANT_COUNT * ADAPTER_RANK).astype(jnp.bfloat16)
    up_gradient = (adapter_scale * jnp.einsum("ohz,ohq->zoq", gradient_blocks, rank_down_values.astype(jnp.float32))).reshape(KEY_VALUE_WIDTH, TENANT_COUNT * ADAPTER_RANK).astype(jnp.bfloat16)
    return input_gradient, down_gradient, up_gradient


def reference(output_gradient, saved_input, frozen_matrix, adapter_down_maps, adapter_up_maps, token_tenants, tenant_slot_lookup):
    inputs_all = []
    downs_all = []
    ups_all = []
    for section_index in range(RELAY_SECTIONS):
        input_gradient, down_gradient, up_gradient = section_gradients(output_gradient[section_index], saved_input[section_index], frozen_matrix[section_index], adapter_down_maps[section_index], adapter_up_maps[section_index], token_tenants[section_index], tenant_slot_lookup[section_index])
        inputs_all.append(input_gradient)
        downs_all.append(down_gradient)
        ups_all.append(up_gradient)
    stacked = jnp.stack(inputs_all)
    passed_grad = jnp.concatenate([stacked[1:], jnp.zeros_like(stacked[:1])], axis=0)
    return passed_grad, jnp.stack(downs_all), jnp.stack(ups_all)
```

```python
import jax
import jax.numpy as jnp
from jax import lax
from jax.experimental import pallas as pl
from jax.experimental.pallas import tpu as pltpu
from jax.sharding import PartitionSpec as P

RANK = 64
WIN = 288
HALF = WIN // 2
PAD = 256
MESH = pl.DeviceIdType.MESH
NT = (((1,), (1,)), ((), ()))
NN = (((1,), (0,)), ((), ()))
TN = (((0,), (0,)), ((), ()))
F32 = jnp.float32
BF16 = jnp.bfloat16


def dot(a, b, dims):
    return lax.dot_general(a, b, dims, preferred_element_type=F32)


def remote(src, dst, send, recv, device):
    return pltpu.make_async_remote_copy(
        src_ref=src, dst_ref=dst, send_sem=send, recv_sem=recv, device_id=device, device_id_type=MESH
    )


def kernel(
    meta, spots, mask, g_hbm, x_hbm, w_ref, at_hbm, ut_ref, passed, da_out, du_out,
    g_all, xf, atf, upad, usib, uexp, p_stage, da_stage, vp, vsib, vrecv, vbf, dubuf, zero,
    loc, ag_s, ag_r, sb_s, sb_r, x_s, x_r, a_s, a_r, us_s, us_r, u_s, u_r, uf_s, uf_r,
    p_s, p_r, da_s, da_r, vs_s, vs_r, v_s, v_r, vb_s, vb_r,
):
    z = lax.axis_index("section")
    me = lax.axis_index("dp")
    last = lax.axis_size("section") - 1
    core = lax.rem(me, 2)
    other = 1 - core
    chip = me // 2
    x, y = chip // 4, lax.rem(chip, 4)
    sib = chip * 2 + other
    width = w_ref.shape[0]
    rows = g_hbm.shape[0]

    def at(dx, dy):
        return lax.rem(x + dx, 4) * 4 + lax.rem(y + dy, 4)

    def start_of(slot):
        return meta[slot] * 16

    def node(p, a, b, who=core):
        return (at(b % 4, a % 4) if p == 0 else at(a % 4, b % 4)) * 2 + who

    def chunk(device, p, part=None):
        first = device * rows + p * 64
        if part is None:
            return g_all.at[pl.ds(pl.multiple_of(first, 64), 64)]
        return g_all.at[pl.ds(pl.multiple_of(first + part * 32, 32), 32)]

    def ag(src, dst, slot, device):
        return remote(src, dst, ag_s.at[slot], ag_r.at[slot], {"dp": device})

    def part_of(d):
        return 0 if d == 1 else 1

    def first(p, d):
        return ag(g_hbm.at[pl.ds(p * 64, 64)], chunk(me, p), p * 20 + part_of(d), node(p, d, 0))

    def got_first(p, d):
        c = chunk(node(p, -d, 0), p)
        ag(c, c, p * 20 + part_of(d), me).wait_recv()

    def fwd1(p, d):
        c = chunk(node(p, -d, 0), p, part_of(d))
        return ag(c, c, p * 20 + 2 + part_of(d), node(p, d, 0))

    def got_fwd1(p, d):
        c = chunk(node(p, 2, 0), p, part_of(d))
        ag(c, c, p * 20 + 2 + part_of(d), me).wait_recv()

    def second(p, q, d):
        c = chunk(node(p, q, 0), p)
        src = g_hbm.at[pl.ds(p * 64, 64)] if q == 0 else c
        return ag(src, c, p * 20 + 4 + q * 4 + part_of(d), node(p, 0, d))

    def got_second(p, q, d):
        c = chunk(node(p, q, -d), p)
        ag(c, c, p * 20 + 4 + q * 4 + part_of(d), me).wait_recv()

    def fwd2(p, q, d):
        c = chunk(node(p, q, -d), p, part_of(d))
        return ag(c, c, p * 20 + 4 + q * 4 + 2 + part_of(d), node(p, 0, d))

    def got_fwd2(p, q, d):
        c = chunk(node(p, q, 2), p, part_of(d))
        ag(c, c, p * 20 + 4 + q * 4 + 2 + part_of(d), me).wait_recv()

    def share(p, a, b, own=False):
        c = chunk(node(p, a, b), p)
        slot = p * 16 + (a % 4) * 4 + b % 4
        src = g_hbm.at[pl.ds(p * 64, 64)] if own else c
        return remote(src, c, sb_s.at[slot], sb_r.at[slot], {"dp": sib})

    def got_share(p, a, b):
        c = chunk(node(p, a, b, other), p)
        slot = p * 16 + (a % 4) * 4 + b % 4
        remote(c, c, sb_s.at[slot], sb_r.at[slot], {"dp": sib}).wait_recv()

    def peer(j):
        return at(j // 8, lax.rem(j // 2, 4)) * 2 + lax.rem(core + lax.rem(j, 2), 2)

    def columns(device):
        return pl.ds(pl.multiple_of(device * width, width), width)

    def x_copy(src_device, dst_device, slot):
        return remote(
            x_hbm.at[:, columns(dst_device)],
            xf.at[pl.ds(pl.multiple_of(src_device * rows, rows), rows)],
            x_s.at[slot], x_r.at[src_device], {"dp": dst_device},
        )

    def a_copy(src_device, dst_device, slot):
        return remote(
            at_hbm.at[:, columns(dst_device)],
            atf.at[pl.ds(pl.multiple_of(src_device * RANK, RANK), RANK)],
            a_s.at[slot], a_r.at[src_device], {"dp": dst_device},
        )

    own_g = pltpu.make_async_copy(g_hbm, g_all.at[pl.ds(pl.multiple_of(me * rows, rows), rows)], loc.at[0])
    own_x = pltpu.make_async_copy(
        x_hbm.at[:, columns(me)], xf.at[pl.ds(pl.multiple_of(me * rows, rows), rows)], loc.at[1]
    )
    own_a = pltpu.make_async_copy(
        at_hbm.at[:, columns(me)], atf.at[pl.ds(pl.multiple_of(me * RANK, RANK), RANK)], loc.at[2]
    )
    dirs = (1, -1)
    for d in dirs:
        for p in range(2):
            first(p, d).start()
    for d in dirs:
        for p in range(2):
            second(p, 0, d).start()
    own_g.start()
    for p in range(2):
        share(p, 0, 0, True).start()

    own_a.start()

    @pl.loop(1, 32)
    def _(j):
        a_copy(me, peer(j), j).start()

    blank = jnp.zeros((16, PAD, 128), BF16)
    upad[:, 0:PAD, :] = blank
    upad[:, PAD + WIN:, :] = blank

    for d in dirs:
        for p in range(2):
            got_first(p, d)
            fwd1(p, d).start()
            for e in dirs:
                second(p, (-d) % 4, e).start()
            share(p, -d, 0).start()
    for d in dirs:
        for p in range(2):
            got_second(p, 0, d)
            fwd2(p, 0, d).start()
            share(p, 0, -d).start()
    for p in range(2):
        for d in dirs:
            got_fwd1(p, d)
        for e in dirs:
            second(p, 2, e).start()
        share(p, 2, 0).start()
    for q in (3, 1):
        for d in dirs:
            for p in range(2):
                got_second(p, q, d)
                fwd2(p, q, d).start()
                share(p, q, -d).start()
    own_x.start()

    @pl.loop(1, 32)
    def _(j):
        x_copy(me, peer(j), j).start()

    for p in range(2):
        for d in dirs:
            got_fwd2(p, 0, d)
        share(p, 0, 2).start()
    for d in dirs:
        for p in range(2):
            got_second(p, 2, d)
            fwd2(p, 2, d).start()
            share(p, 2, -d).start()
    for q in (3, 1, 2):
        for p in range(2):
            for d in dirs:
                got_fwd2(p, q, d)
            share(p, q, 2).start()
    own_g.wait()
    for p in range(2):
        for a in range(4):
            for b in range(4):
                got_share(p, a, b)

    s0 = start_of(me)
    lane = lax.broadcasted_iota(jnp.int32, (WIN, 128), 1)
    ut2 = jnp.concatenate([ut_ref[...], ut_ref[...]], axis=0)
    u_own = (mask[...] * dot(g_all[pl.ds(s0, WIN), :], ut2, NT)).astype(BF16)
    usib[0] = u_own
    to_sib = remote(usib.at[0], usib.at[1], us_s, us_r, {"dp": sib})
    to_sib.start()
    to_sib.wait_recv()
    upad[chip, PAD:PAD + WIN, :] = u_own + usib[1]

    def u_rows(c, part):
        return upad.at[c, pl.ds(pl.multiple_of(PAD + part * HALF, 16), HALF)]

    def u_copy(c, device):
        return remote(u_rows(c, core), u_rows(c, core), u_s.at[device // 2], u_r.at[c], {"dp": device})

    def u_share(c, part):
        return remote(u_rows(c, part), u_rows(c, part), uf_s.at[c], uf_r.at[c], {"dp": sib})

    def chip_at(j):
        return at(j // 4, lax.rem(j, 4))

    @pl.loop(1, 16)
    def _(j):
        u_copy(chip, chip_at(j) * 2 + core).start()

    own_a.wait()

    @pl.loop(1, 32)
    def _(j):
        a_copy(peer(j), me, j).wait_recv()

    @pl.loop(1, 16)
    def _(j):
        c = chip_at(j)
        u_copy(c, c * 2 + core).wait_recv()
        u_share(c, core).start()

    @pl.loop(1, 16)
    def _(j):
        u_share(chip_at(j), other).wait_recv()

    def p_copy(src_device, dst_device):
        return remote(
            p_stage.at[pl.ds(pl.multiple_of(dst_device * rows, rows), rows)],
            passed.at[:, columns(src_device)],
            p_s.at[dst_device], p_r.at[src_device], {"section": lax.rem(z + last, last + 1), "dp": dst_device},
        )

    low = (lax.broadcasted_iota(jnp.int32, (2 * rows, 128), 1) < RANK).astype(F32).astype(BF16)
    high = (lax.broadcasted_iota(jnp.int32, (2 * rows, 128), 1) >= RANK).astype(F32).astype(BF16)

    @pl.when(z > 0)
    def _():
        @pl.loop(0, 16)
        def _(j):
            c = chip_at(j)
            base = pl.multiple_of(c * 2 * rows, 2 * rows)
            for k in range(16):
                even = spots[c * 32 + 2 * k] * 16
                odd = spots[c * 32 + 2 * k + 1] * 16
                uexp[:, k * 128:(k + 1) * 128] = (
                    upad[k, pl.ds(even, 2 * rows), :] * low
                    + upad[k, pl.ds(odd, 2 * rows), :] * high
                )
            tile = dot(g_all[pl.ds(base, 2 * rows), :], w_ref[...], NT)
            tile = tile + 2.0 * dot(uexp[...], atf[...], NN)
            p_stage[pl.ds(base, 2 * rows), :] = tile.astype(BF16)
            p_copy(me, c * 2 + core).start()
            p_copy(me, c * 2 + other).start()

    @pl.when(z == last)
    def _():
        zero[...] = jnp.zeros_like(zero)

        @pl.loop(0, 32)
        def _(j):
            pltpu.make_async_copy(zero, passed.at[:, columns(j)], p_r.at[j]).start()

    own_x.wait()

    @pl.loop(1, 32)
    def _(j):
        x_copy(peer(j), me, j).wait_recv()

    def da_copy(src_device, dst_device):
        return remote(
            da_stage.at[pl.ds(pl.multiple_of(dst_device * RANK, RANK), RANK)],
            da_out.at[:, columns(src_device)],
            da_s.at[dst_device], da_r.at[src_device], {"dp": dst_device},
        )

    own_da = pltpu.make_async_copy(
        da_stage.at[pl.ds(pl.multiple_of(me * RANK, RANK), RANK)], da_out.at[:, columns(me)], loc.at[3]
    )

    @pl.loop(0, 16)
    def _(j):
        c = chip_at(j)
        xe = xf[pl.ds(start_of(2 * c), WIN), :]
        xo = xf[pl.ds(start_of(2 * c + 1), WIN), :]
        pair = atf[pl.ds(pl.multiple_of(c * 128, 128), 128), :]
        vp[c] = jnp.where(lane < RANK, dot(xe, pair, NT), dot(xo, pair, NT))
        u = upad[c, PAD:PAD + WIN, :]
        grad_row = lax.broadcasted_iota(jnp.int32, (128, width), 0)
        da = jnp.where(grad_row < RANK, dot(u, xe, TN), dot(u, xo, TN))
        da_stage[pl.ds(pl.multiple_of(c * 128, 128), 128), :] = (2.0 * da).astype(BF16)

        @pl.when(j == 0)
        def _():
            own_da.start()

        @pl.when(j > 0)
        def _():
            da_copy(me, c * 2 + core).start()

        da_copy(me, c * 2 + other).start()

    def half(part):
        return pl.ds(pl.multiple_of(part * HALF, 8), HALF)

    v_swap = remote(vp.at[:, half(other)], vsib, vs_s, vs_r, {"dp": sib})
    v_swap.start()
    v_swap.wait_recv()

    def v_copy(src_chip, dst_chip):
        return remote(vsib.at[dst_chip], vrecv.at[src_chip], v_s.at[dst_chip], v_r.at[src_chip], {"dp": dst_chip * 2 + core})

    @pl.loop(1, 16)
    def _(j):
        c = chip_at(j)
        vsib[c] = vsib[c] + vp[c, half(core), :]
        v_copy(chip, c).start()

    total = vsib[chip] + vp[chip, half(core), :]

    def add(j, total):
        c = chip_at(j)
        v_copy(c, chip).wait_recv()
        return total + vrecv[c]

    vbf[half_bf(core), :] = lax.fori_loop(1, 16, add, total).astype(BF16)
    v_back = remote(vbf.at[half_bf(core)], vbf.at[half_bf(core)], vb_s, vb_r, {"dp": sib})
    v_back.start()
    remote(vbf.at[half_bf(other)], vbf.at[half_bf(other)], vb_s, vb_r, {"dp": sib}).wait_recv()
    v = (mask[...] * vbf[...].astype(F32)).astype(BF16)

    @pl.loop(0, 4)
    def _(i):
        part = pl.ds(pl.multiple_of(i * 512, 512), 512)
        dubuf[:, part] = (2.0 * dot(v, g_all[pl.ds(s0, WIN), part], TN)).astype(BF16)

    own_du = pltpu.make_async_copy(dubuf.at[pl.ds(pl.multiple_of(core * RANK, RANK), RANK)], du_out, loc.at[4])
    own_du.start()

    own_da.wait()
    own_du.wait()
    to_sib.wait_send()
    v_swap.wait_send()
    v_back.wait_send()
    for p in range(2):
        for d in dirs:
            first(p, d).wait_send()
            fwd1(p, d).wait_send()
            for q in range(4):
                second(p, q, d).wait_send()
                fwd2(p, q, d).wait_send()
        for a in range(4):
            for b in range(4):
                share(p, a, b).wait_send()

    @pl.loop(1, 32)
    def _(j):
        d = peer(j)
        a_copy(me, d, j).wait_send()
        x_copy(me, d, j).wait_send()
        da_copy(me, d).wait_send()
        da_copy(d, me).wait_recv()

    @pl.loop(1, 16)
    def _(j):
        c = chip_at(j)
        u_copy(chip, c * 2 + core).wait_send()
        u_share(c, core).wait_send()
        v_copy(chip, c).wait_send()

    @pl.when(z > 0)
    def _():
        @pl.loop(0, 32)
        def _(j):
            p_copy(me, j).wait_send()

    @pl.when(z < last)
    def _():
        @pl.loop(0, 32)
        def _(j):
            p_copy(j, me).wait_recv()

    @pl.when(z == last)
    def _():
        @pl.loop(0, 32)
        def _(j):
            pltpu.make_async_copy(zero, passed.at[:, columns(j)], p_r.at[j]).wait()


def half_bf(part):
    return pl.ds(pl.multiple_of(part * HALF, 16), HALF)


def local(output_gradient, saved_input, frozen_matrix, down_maps, up_maps, token_tenants, slot_lookup):
    tokens = token_tenants.shape[1]
    tenants = slot_lookup.shape[1]
    order = jnp.arange(tenants, dtype=jnp.int32)
    tenant_of = jnp.sum(jnp.where(slot_lookup[0][None, :] == order[:, None], order[None, :], 0), axis=1)
    row = token_tenants[0][None, :]
    start = jnp.sum((row < tenant_of[:, None]).astype(jnp.int32), axis=1)
    count = jnp.sum((row == tenant_of[:, None]).astype(jnp.int32), axis=1)
    meta = jnp.minimum(start // 16, (tokens - WIN) // 16)
    block = jnp.arange(16, dtype=jnp.int32) * (tokens // 256)
    spots = jnp.clip(PAD // 16 + block[:, None] - meta[None, :], 0, (PAD + WIN) // 16).reshape(-1)
    me = lax.axis_index("dp")
    place = jnp.arange(WIN, dtype=jnp.int32)[:, None]
    begin, size, first = (jnp.sum(jnp.where(order == me, t, 0)) for t in (start, count, meta * 16))
    side = jnp.arange(128, dtype=jnp.int32)[None, :] // RANK
    live = (place >= begin - first) & (place < begin - first + size) & (side == me % 2)
    mask = live.astype(F32)

    rows, kv = output_gradient.shape[1:]
    model = saved_input.shape[2]
    width = frozen_matrix.shape[1]
    hbm = pl.BlockSpec(memory_space=pl.ANY)
    vmem = pl.BlockSpec(memory_space=pltpu.VMEM)
    smem = pl.BlockSpec(memory_space=pltpu.SMEM)
    dma = pltpu.SemaphoreType.DMA
    passed, da, du = pl.pallas_call(
        kernel,
        out_shape=(
            jax.ShapeDtypeStruct((rows, model), BF16),
            jax.ShapeDtypeStruct((RANK, model), BF16),
            jax.ShapeDtypeStruct((RANK, kv), BF16),
        ),
        in_specs=[smem, smem, vmem, hbm, hbm, vmem, hbm, vmem],
        out_specs=(hbm, hbm, hbm),
        scratch_shapes=[
            pltpu.VMEM((tokens, kv), BF16),
            pltpu.VMEM((tokens, width), BF16),
            pltpu.VMEM((tenants * RANK, width), BF16),
            pltpu.VMEM((16, PAD + WIN + PAD, 128), BF16),
            pltpu.VMEM((2, WIN, 128), BF16),
            pltpu.VMEM((2 * rows, tenants * RANK), BF16),
            pltpu.VMEM((tokens, width), BF16),
            pltpu.VMEM((tenants * RANK, width), BF16),
            pltpu.VMEM((16, WIN, 128), F32),
            pltpu.VMEM((16, HALF, 128), F32),
            pltpu.VMEM((16, HALF, 128), F32),
            pltpu.VMEM((WIN, 128), BF16),
            pltpu.VMEM((128, kv), BF16),
            pltpu.VMEM((rows, width), BF16),
            dma((5,)),
            dma((40,)), dma((40,)), dma((32,)), dma((32,)),
            dma((32,)), dma((32,)), dma((32,)), dma((32,)),
            dma, dma, dma((16,)), dma((16,)), dma((16,)), dma((16,)),
            dma((32,)), dma((32,)), dma((32,)), dma((32,)),
            dma, dma, dma((16,)), dma((16,)), dma, dma,
        ],
        compiler_params=pltpu.CompilerParams(has_side_effects=True, vmem_limit_bytes=56 << 20),
    )(
        meta,
        spots,
        mask,
        output_gradient[0],
        saved_input[0],
        frozen_matrix[0],
        jnp.swapaxes(down_maps[0], 0, 1),
        jnp.swapaxes(up_maps[0], 0, 1),
    )
    return passed[None], jnp.swapaxes(da, 0, 1)[None], jnp.swapaxes(du, 0, 1)[None]


def solution(mesh):
    return jax.shard_map(
        local,
        mesh=mesh,
        in_specs=(
            P("section", "dp", None),
            P("section", "dp", None),
            P("section", "dp", None),
            P("section", None, "dp"),
            P("section", None, "dp"),
            P("section", None),
            P("section", None),
        ),
        out_specs=(P("section", "dp", None), P("section", None, "dp"), P("section", None, "dp")),
        check_vma=False,
    )
```

```python
import jax
import jax.numpy as jnp
from jax import lax
from jax.experimental import pallas as pl
from jax.experimental.pallas import tpu as pltpu
from jax.sharding import PartitionSpec as P

RANK = 64
WIN = 288
HALF = WIN // 2
PAD = 256
MESH = pl.DeviceIdType.MESH
NT = (((1,), (1,)), ((), ()))
NN = (((1,), (0,)), ((), ()))
TN = (((0,), (0,)), ((), ()))
F32 = jnp.float32
BF16 = jnp.bfloat16


def dot(a, b, dims):
    return lax.dot_general(a, b, dims, preferred_element_type=F32)


def remote(src, dst, send, recv, device):
    return pltpu.make_async_remote_copy(
        src_ref=src, dst_ref=dst, send_sem=send, recv_sem=recv, device_id=device, device_id_type=MESH
    )


def kernel(
    meta, spots, mask, g_hbm, x_hbm, w_ref, at_hbm, ut_ref, passed, da_out, du_out,
    g_all, xf, atf, upad, usib, uexp, p_stage, da_stage, vp, vsib, vrecv, vbf, dubuf, zero,
    ready, loc, ag_s, ag_r, sb_s, sb_r, x_s, x_r, a_s, a_r, us_s, us_r, u_s, u_r, uf_s, uf_r,
    p_s, p_r, da_s, da_r, vs_s, vs_r, v_s, v_r, vb_s, vb_r,
):
    z = lax.axis_index("section")
    me = lax.axis_index("dp")
    last = lax.axis_size("section") - 1
    core = lax.rem(me, 2)
    other = 1 - core
    chip = me // 2
    x, y = chip // 4, lax.rem(chip, 4)
    sib = chip * 2 + other
    width = w_ref.shape[0]
    rows = g_hbm.shape[0]

    def at(dx, dy):
        return lax.rem(x + dx, 4) * 4 + lax.rem(y + dy, 4)

    def start_of(slot):
        return meta[slot] * 16

    sections = last + 1
    barrier = pltpu.get_barrier_semaphore()

    @pl.loop(1, 32)
    def _(j):
        pl.semaphore_signal(barrier, 1, device_id={"dp": lax.rem(me + j, 32)}, device_id_type=MESH)

    for step in (1, last):
        pl.semaphore_signal(barrier, 1, device_id={"section": lax.rem(z + step, sections)}, device_id_type=MESH)
    pl.semaphore_wait(barrier, 33)
    pl.semaphore_signal(ready, 1, device_id={"section": lax.rem(z + 1, sections)}, device_id_type=MESH)

    def node(p, a, b, who=core):
        return (at(b % 4, a % 4) if p == 0 else at(a % 4, b % 4)) * 2 + who

    def chunk(device, p, part=None):
        first = device * rows + p * 64
        if part is None:
            return g_all.at[pl.ds(pl.multiple_of(first, 64), 64)]
        return g_all.at[pl.ds(pl.multiple_of(first + part * 32, 32), 32)]

    def ag(src, dst, slot, device):
        return remote(src, dst, ag_s.at[slot], ag_r.at[slot], {"dp": device})

    def part_of(d):
        return 0 if d == 1 else 1

    def first(p, d):
        return ag(g_hbm.at[pl.ds(p * 64, 64)], chunk(me, p), p * 20 + part_of(d), node(p, d, 0))

    def got_first(p, d):
        c = chunk(node(p, -d, 0), p)
        ag(c, c, p * 20 + part_of(d), me).wait_recv()

    def fwd1(p, d):
        c = chunk(node(p, -d, 0), p, part_of(d))
        return ag(c, c, p * 20 + 2 + part_of(d), node(p, d, 0))

    def got_fwd1(p, d):
        c = chunk(node(p, 2, 0), p, part_of(d))
        ag(c, c, p * 20 + 2 + part_of(d), me).wait_recv()

    def second(p, q, d):
        c = chunk(node(p, q, 0), p)
        src = g_hbm.at[pl.ds(p * 64, 64)] if q == 0 else c
        return ag(src, c, p * 20 + 4 + q * 4 + part_of(d), node(p, 0, d))

    def got_second(p, q, d):
        c = chunk(node(p, q, -d), p)
        ag(c, c, p * 20 + 4 + q * 4 + part_of(d), me).wait_recv()

    def fwd2(p, q, d):
        c = chunk(node(p, q, -d), p, part_of(d))
        return ag(c, c, p * 20 + 4 + q * 4 + 2 + part_of(d), node(p, 0, d))

    def got_fwd2(p, q, d):
        c = chunk(node(p, q, 2), p, part_of(d))
        ag(c, c, p * 20 + 4 + q * 4 + 2 + part_of(d), me).wait_recv()

    def share(p, a, b, own=False):
        c = chunk(node(p, a, b), p)
        slot = p * 16 + (a % 4) * 4 + b % 4
        src = g_hbm.at[pl.ds(p * 64, 64)] if own else c
        return remote(src, c, sb_s.at[slot], sb_r.at[slot], {"dp": sib})

    def got_share(p, a, b):
        c = chunk(node(p, a, b, other), p)
        slot = p * 16 + (a % 4) * 4 + b % 4
        remote(c, c, sb_s.at[slot], sb_r.at[slot], {"dp": sib}).wait_recv()

    def chip_at(j):
        return at(lax.rem(j, 4), lax.rem(j + j // 4, 4))

    def peer(j):
        return chip_at(j // 2) * 2 + lax.rem(core + lax.rem(j, 2), 2)

    def columns(device):
        return pl.ds(pl.multiple_of(device * width, width), width)

    def x_copy(src_device, dst_device, slot):
        return remote(
            x_hbm.at[:, columns(dst_device)],
            xf.at[pl.ds(pl.multiple_of(src_device * rows, rows), rows)],
            x_s.at[slot], x_r.at[src_device], {"dp": dst_device},
        )

    def a_copy(src_device, dst_device, slot):
        return remote(
            at_hbm.at[:, columns(dst_device)],
            atf.at[pl.ds(pl.multiple_of(src_device * RANK, RANK), RANK)],
            a_s.at[slot], a_r.at[src_device], {"dp": dst_device},
        )

    own_g = pltpu.make_async_copy(g_hbm, g_all.at[pl.ds(pl.multiple_of(me * rows, rows), rows)], loc.at[0])
    own_x = pltpu.make_async_copy(
        x_hbm.at[:, columns(me)], xf.at[pl.ds(pl.multiple_of(me * rows, rows), rows)], loc.at[1]
    )
    own_a = pltpu.make_async_copy(
        at_hbm.at[:, columns(me)], atf.at[pl.ds(pl.multiple_of(me * RANK, RANK), RANK)], loc.at[2]
    )
    dirs = (1, -1)
    for d in dirs:
        for p in range(2):
            first(p, d).start()
    for d in dirs:
        for p in range(2):
            second(p, 0, d).start()
    own_g.start()
    for p in range(2):
        share(p, 0, 0, True).start()

    own_a.start()

    @pl.loop(1, 32)
    def _(j):
        a_copy(me, peer(j), j).start()

    blank = jnp.zeros((16, PAD, 128), BF16)
    upad[:, 0:PAD, :] = blank
    upad[:, PAD + WIN:, :] = blank

    for d in dirs:
        for p in range(2):
            got_first(p, d)
            fwd1(p, d).start()
            for e in dirs:
                second(p, (-d) % 4, e).start()
            share(p, -d, 0).start()
    for d in dirs:
        for p in range(2):
            got_second(p, 0, d)
            fwd2(p, 0, d).start()
            share(p, 0, -d).start()
    for p in range(2):
        for d in dirs:
            got_fwd1(p, d)
        for e in dirs:
            second(p, 2, e).start()
        share(p, 2, 0).start()
    for q in (3, 1):
        for d in dirs:
            for p in range(2):
                got_second(p, q, d)
                fwd2(p, q, d).start()
                share(p, q, -d).start()
    own_x.start()

    @pl.loop(1, 32)
    def _(j):
        x_copy(me, peer(j), j).start()

    for p in range(2):
        for d in dirs:
            got_fwd2(p, 0, d)
        share(p, 0, 2).start()
    for d in dirs:
        for p in range(2):
            got_second(p, 2, d)
            fwd2(p, 2, d).start()
            share(p, 2, -d).start()
    for q in (3, 1, 2):
        for p in range(2):
            for d in dirs:
                got_fwd2(p, q, d)
            share(p, q, 2).start()
    own_g.wait()
    for p in range(2):
        for a in range(4):
            for b in range(4):
                got_share(p, a, b)

    s0 = start_of(me)
    lane = lax.broadcasted_iota(jnp.int32, (WIN, 128), 1)
    ut2 = jnp.concatenate([ut_ref[...], ut_ref[...]], axis=0)
    u_own = (mask[...] * dot(g_all[pl.ds(s0, WIN), :], ut2, NT)).astype(BF16)
    usib[0] = u_own
    to_sib = remote(usib.at[0], usib.at[1], us_s, us_r, {"dp": sib})
    to_sib.start()
    to_sib.wait_recv()
    upad[chip, PAD:PAD + WIN, :] = u_own + usib[1]

    def u_rows(c, part):
        return upad.at[c, pl.ds(pl.multiple_of(PAD + part * HALF, 16), HALF)]

    def u_copy(c, device):
        return remote(u_rows(c, core), u_rows(c, core), u_s.at[device // 2], u_r.at[c], {"dp": device})

    def u_share(c, part):
        return remote(u_rows(c, part), u_rows(c, part), uf_s.at[c], uf_r.at[c], {"dp": sib})

    @pl.loop(1, 16)
    def _(j):
        u_copy(chip, chip_at(j) * 2 + core).start()

    own_a.wait()

    @pl.loop(1, 32)
    def _(j):
        a_copy(peer(j), me, j).wait_recv()

    own_x.wait()

    @pl.loop(1, 32)
    def _(j):
        x_copy(peer(j), me, j).wait_recv()

    @pl.loop(0, 16)
    def _(c):
        pair = atf[pl.ds(pl.multiple_of(c * 128, 128), 128), :]
        even = dot(xf[pl.ds(start_of(2 * c), WIN), :], pair, NT)
        odd = dot(xf[pl.ds(start_of(2 * c + 1), WIN), :], pair, NT)
        vp[c] = jnp.where(lane < RANK, even, odd)

    def half(part):
        return pl.ds(pl.multiple_of(part * HALF, 8), HALF)

    v_swap = remote(vp.at[:, half(other)], vsib, vs_s, vs_r, {"dp": sib})
    v_swap.start()

    @pl.loop(1, 16)
    def _(j):
        c = chip_at(j)
        u_copy(c, c * 2 + core).wait_recv()
        u_share(c, core).start()

    def v_copy(src_chip, dst_chip):
        return remote(vsib.at[dst_chip], vrecv.at[src_chip], v_s.at[dst_chip], v_r.at[src_chip], {"dp": dst_chip * 2 + core})

    v_swap.wait_recv()

    @pl.loop(1, 16)
    def _(j):
        c = chip_at(j)
        vsib[c] = vsib[c] + vp[c, half(core), :]
        v_copy(chip, c).start()

    @pl.loop(1, 16)
    def _(j):
        u_share(chip_at(j), other).wait_recv()

    pl.semaphore_wait(ready, 1)

    def p_copy(src_device, dst_device):
        return remote(
            p_stage.at[pl.ds(pl.multiple_of(dst_device * rows, rows), rows)],
            passed.at[:, columns(src_device)],
            p_s.at[dst_device], p_r.at[src_device], {"section": lax.rem(z + last, last + 1), "dp": dst_device},
        )

    low = (lax.broadcasted_iota(jnp.int32, (2 * rows, 128), 1) < RANK).astype(F32).astype(BF16)
    high = (lax.broadcasted_iota(jnp.int32, (2 * rows, 128), 1) >= RANK).astype(F32).astype(BF16)

    def da_copy(src_device, dst_device):
        return remote(
            da_stage.at[pl.ds(pl.multiple_of(dst_device * RANK, RANK), RANK)],
            da_out.at[:, columns(src_device)],
            da_s.at[dst_device], da_r.at[src_device], {"dp": dst_device},
        )

    own_da = pltpu.make_async_copy(
        da_stage.at[pl.ds(pl.multiple_of(me * RANK, RANK), RANK)], da_out.at[:, columns(me)], loc.at[3]
    )

    @pl.loop(0, 16)
    def _(j):
        c = chip_at(j)

        @pl.when(z > 0)
        def _():
            base = pl.multiple_of(c * 2 * rows, 2 * rows)
            for k in range(16):
                even = spots[c * 32 + 2 * k] * 16
                odd = spots[c * 32 + 2 * k + 1] * 16
                uexp[:, k * 128:(k + 1) * 128] = (
                    upad[k, pl.ds(even, 2 * rows), :] * low + upad[k, pl.ds(odd, 2 * rows), :] * high
                )
            tile = dot(g_all[pl.ds(base, 2 * rows), :], w_ref[...], NT)
            tile = tile + 2.0 * dot(uexp[...], atf[...], NN)
            p_stage[pl.ds(base, 2 * rows), :] = tile.astype(BF16)
            p_copy(me, c * 2 + core).start()
            p_copy(me, c * 2 + other).start()

        u = upad[c, PAD:PAD + WIN, :]
        even = dot(u, xf[pl.ds(start_of(2 * c), WIN), :], TN)
        odd = dot(u, xf[pl.ds(start_of(2 * c + 1), WIN), :], TN)
        grad_row = lax.broadcasted_iota(jnp.int32, (128, width), 0)
        da_stage[pl.ds(pl.multiple_of(c * 128, 128), 128), :] = (
            2.0 * jnp.where(grad_row < RANK, even, odd)
        ).astype(BF16)

        @pl.when(j == 0)
        def _():
            own_da.start()

        @pl.when(j > 0)
        def _():
            da_copy(me, c * 2 + core).start()

        da_copy(me, c * 2 + other).start()

    @pl.when(z == last)
    def _():
        zero[...] = jnp.zeros_like(zero)

        @pl.loop(0, 32)
        def _(j):
            pltpu.make_async_copy(zero, passed.at[:, columns(j)], p_r.at[j]).start()

    total = vsib[chip] + vp[chip, half(core), :]

    def add(j, total):
        c = chip_at(j)
        v_copy(c, chip).wait_recv()
        return total + vrecv[c]

    vbf[half_bf(core), :] = lax.fori_loop(1, 16, add, total).astype(BF16)
    v_back = remote(vbf.at[half_bf(core)], vbf.at[half_bf(core)], vb_s, vb_r, {"dp": sib})
    v_back.start()
    remote(vbf.at[half_bf(other)], vbf.at[half_bf(other)], vb_s, vb_r, {"dp": sib}).wait_recv()
    v = (mask[...] * vbf[...].astype(F32)).astype(BF16)

    @pl.loop(0, 4)
    def _(i):
        part = pl.ds(pl.multiple_of(i * 512, 512), 512)
        dubuf[:, part] = (2.0 * dot(v, g_all[pl.ds(s0, WIN), part], TN)).astype(BF16)

    own_du = pltpu.make_async_copy(dubuf.at[pl.ds(pl.multiple_of(core * RANK, RANK), RANK)], du_out, loc.at[4])
    own_du.start()

    own_da.wait()
    own_du.wait()
    to_sib.wait_send()
    v_swap.wait_send()
    v_back.wait_send()
    for p in range(2):
        for d in dirs:
            first(p, d).wait_send()
            fwd1(p, d).wait_send()
            for q in range(4):
                second(p, q, d).wait_send()
                fwd2(p, q, d).wait_send()
        for a in range(4):
            for b in range(4):
                share(p, a, b).wait_send()

    @pl.loop(1, 32)
    def _(j):
        d = peer(j)
        a_copy(me, d, j).wait_send()
        x_copy(me, d, j).wait_send()
        da_copy(me, d).wait_send()
        da_copy(d, me).wait_recv()

    @pl.loop(1, 16)
    def _(j):
        c = chip_at(j)
        u_copy(chip, c * 2 + core).wait_send()
        u_share(c, core).wait_send()
        v_copy(chip, c).wait_send()

    @pl.when(z > 0)
    def _():
        @pl.loop(0, 32)
        def _(j):
            p_copy(me, j).wait_send()

    @pl.when(z < last)
    def _():
        @pl.loop(0, 32)
        def _(j):
            p_copy(j, me).wait_recv()

    @pl.when(z == last)
    def _():
        @pl.loop(0, 32)
        def _(j):
            pltpu.make_async_copy(zero, passed.at[:, columns(j)], p_r.at[j]).wait()


def half_bf(part):
    return pl.ds(pl.multiple_of(part * HALF, 16), HALF)


def local(output_gradient, saved_input, frozen_matrix, down_maps, up_maps, token_tenants, slot_lookup):
    tokens = token_tenants.shape[1]
    tenants = slot_lookup.shape[1]
    order = jnp.arange(tenants, dtype=jnp.int32)
    tenant_of = jnp.sum(jnp.where(slot_lookup[0][None, :] == order[:, None], order[None, :], 0), axis=1)
    row = token_tenants[0][None, :]
    start = jnp.sum((row < tenant_of[:, None]).astype(jnp.int32), axis=1)
    count = jnp.sum((row == tenant_of[:, None]).astype(jnp.int32), axis=1)
    meta = jnp.minimum(start // 16, (tokens - WIN) // 16)
    block = jnp.arange(16, dtype=jnp.int32) * (tokens // 256)
    spots = jnp.clip(PAD // 16 + block[:, None] - meta[None, :], 0, (PAD + WIN) // 16).reshape(-1)
    me = lax.axis_index("dp")
    place = jnp.arange(WIN, dtype=jnp.int32)[:, None]
    begin, size, first = (jnp.sum(jnp.where(order == me, t, 0)) for t in (start, count, meta * 16))
    side = jnp.arange(128, dtype=jnp.int32)[None, :] // RANK
    live = (place >= begin - first) & (place < begin - first + size) & (side == me % 2)
    mask = live.astype(F32)

    rows, kv = output_gradient.shape[1:]
    model = saved_input.shape[2]
    width = frozen_matrix.shape[1]
    hbm = pl.BlockSpec(memory_space=pl.ANY)
    vmem = pl.BlockSpec(memory_space=pltpu.VMEM)
    smem = pl.BlockSpec(memory_space=pltpu.SMEM)
    dma = pltpu.SemaphoreType.DMA
    passed, da, du = pl.pallas_call(
        kernel,
        out_shape=(
            jax.ShapeDtypeStruct((rows, model), BF16),
            jax.ShapeDtypeStruct((RANK, model), BF16),
            jax.ShapeDtypeStruct((RANK, kv), BF16),
        ),
        in_specs=[smem, smem, vmem, hbm, hbm, vmem, hbm, vmem],
        out_specs=(hbm, hbm, hbm),
        scratch_shapes=[
            pltpu.VMEM((tokens, kv), BF16),
            pltpu.VMEM((tokens, width), BF16),
            pltpu.VMEM((tenants * RANK, width), BF16),
            pltpu.VMEM((16, PAD + WIN + PAD, 128), BF16),
            pltpu.VMEM((2, WIN, 128), BF16),
            pltpu.VMEM((2 * rows, tenants * RANK), BF16),
            pltpu.VMEM((tokens, width), BF16),
            pltpu.VMEM((tenants * RANK, width), BF16),
            pltpu.VMEM((16, WIN, 128), F32),
            pltpu.VMEM((16, HALF, 128), F32),
            pltpu.VMEM((16, HALF, 128), F32),
            pltpu.VMEM((WIN, 128), BF16),
            pltpu.VMEM((128, kv), BF16),
            pltpu.VMEM((rows, width), BF16),
            pltpu.SemaphoreType.REGULAR,
            dma((5,)),
            dma((40,)), dma((40,)), dma((32,)), dma((32,)),
            dma((32,)), dma((32,)), dma((32,)), dma((32,)),
            dma, dma, dma((16,)), dma((16,)), dma((16,)), dma((16,)),
            dma((32,)), dma((32,)), dma((32,)), dma((32,)),
            dma, dma, dma((16,)), dma((16,)), dma, dma,
        ],
        compiler_params=pltpu.CompilerParams(collective_id=0, has_side_effects=True, vmem_limit_bytes=56 << 20),
    )(
        meta,
        spots,
        mask,
        output_gradient[0],
        saved_input[0],
        frozen_matrix[0],
        jnp.swapaxes(down_maps[0], 0, 1),
        jnp.swapaxes(up_maps[0], 0, 1),
    )
    return passed[None], jnp.swapaxes(da, 0, 1)[None], jnp.swapaxes(du, 0, 1)[None]


def solution(mesh):
    return jax.shard_map(
        local,
        mesh=mesh,
        in_specs=(
            P("section", "dp", None),
            P("section", "dp", None),
            P("section", "dp", None),
            P("section", None, "dp"),
            P("section", None, "dp"),
            P("section", None),
            P("section", None),
        ),
        out_specs=(P("section", "dp", None), P("section", None, "dp"), P("section", None, "dp")),
        check_vma=False,
    )
```

```python
import jax
import jax.numpy as jnp
from jax import lax
from jax.experimental import pallas as pl
from jax.experimental.pallas import tpu as pltpu
from jax.sharding import PartitionSpec as P

RANK = 64
WIN = 288
HALF = WIN // 2
PAD = 256
MESH = pl.DeviceIdType.MESH
NT = (((1,), (1,)), ((), ()))
NN = (((1,), (0,)), ((), ()))
TN = (((0,), (0,)), ((), ()))
F32 = jnp.float32
BF16 = jnp.bfloat16


def dot(a, b, dims):
    return lax.dot_general(a, b, dims, preferred_element_type=F32)


def remote(src, dst, send, recv, device):
    return pltpu.make_async_remote_copy(
        src_ref=src, dst_ref=dst, send_sem=send, recv_sem=recv, device_id=device, device_id_type=MESH
    )


def kernel(
    meta, spots, mask, g_hbm, x_hbm, w_ref, at_hbm, ut_ref, passed, da_out, du_out,
    g_all, xf, atf, upad, usib, uexp, p_stage, da_stage, vp, vsib, vrecv, vbf, dubuf, zero,
    ready, loc, ag_s, ag_r, sb_s, sb_r, x_s, x_r, a_s, a_r, us_s, us_r, u_s, u_r, uf_s, uf_r,
    p_s, p_r, da_s, da_r, vs_s, vs_r, v_s, v_r, vb_s, vb_r,
):
    z = lax.axis_index("section")
    me = lax.axis_index("dp")
    last = lax.axis_size("section") - 1
    core = me & 1
    other = core ^ 1
    chip = me >> 1
    sib = me ^ 1
    along_x = [((me >> 3) + d & 3) * 8 for d in range(4)]
    along_y = [(chip + d & 3) * 2 for d in range(4)]
    after = jnp.where(z == last, 0, z + 1)
    before = jnp.where(z == 0, last, z - 1)
    width = w_ref.shape[0]
    rows = g_hbm.shape[0]

    def start_of(slot):
        return meta[slot] * 16

    barrier = pltpu.get_barrier_semaphore()

    @pl.loop(1, 32)
    def _(j):
        pl.semaphore_signal(barrier, 1, device_id={"dp": me ^ j}, device_id_type=MESH)

    for section in (after, before):
        pl.semaphore_signal(barrier, 1, device_id={"section": section}, device_id_type=MESH)
    pl.semaphore_wait(barrier, 33)
    pl.semaphore_signal(ready, 1, device_id={"section": after}, device_id_type=MESH)

    def node(p, a, b, who=core):
        dx, dy = (b, a) if p == 0 else (a, b)
        return along_x[dx % 4] + along_y[dy % 4] + who

    def chunk(device, p, part=None):
        first = device * rows + p * 64
        if part is None:
            return g_all.at[pl.ds(pl.multiple_of(first, 64), 64)]
        return g_all.at[pl.ds(pl.multiple_of(first + part * 32, 32), 32)]

    def ag(src, dst, slot, device):
        return remote(src, dst, ag_s.at[slot], ag_r.at[slot], {"dp": device})

    def part_of(d):
        return 0 if d == 1 else 1

    def first(p, d):
        return ag(g_hbm.at[pl.ds(p * 64, 64)], chunk(me, p), p * 20 + part_of(d), node(p, d, 0))

    def got_first(p, d):
        c = chunk(node(p, -d, 0), p)
        ag(c, c, p * 20 + part_of(d), me).wait_recv()

    def fwd1(p, d):
        c = chunk(node(p, -d, 0), p, part_of(d))
        return ag(c, c, p * 20 + 2 + part_of(d), node(p, d, 0))

    def got_fwd1(p, d):
        c = chunk(node(p, 2, 0), p, part_of(d))
        ag(c, c, p * 20 + 2 + part_of(d), me).wait_recv()

    def second(p, q, d):
        c = chunk(node(p, q, 0), p)
        src = g_hbm.at[pl.ds(p * 64, 64)] if q == 0 else c
        return ag(src, c, p * 20 + 4 + q * 4 + part_of(d), node(p, 0, d))

    def got_second(p, q, d):
        c = chunk(node(p, q, -d), p)
        ag(c, c, p * 20 + 4 + q * 4 + part_of(d), me).wait_recv()

    def fwd2(p, q, d):
        c = chunk(node(p, q, -d), p, part_of(d))
        return ag(c, c, p * 20 + 4 + q * 4 + 2 + part_of(d), node(p, 0, d))

    def got_fwd2(p, q, d):
        c = chunk(node(p, q, 2), p, part_of(d))
        ag(c, c, p * 20 + 4 + q * 4 + 2 + part_of(d), me).wait_recv()

    def share(p, a, b, own=False):
        c = chunk(node(p, a, b), p)
        slot = p * 16 + (a % 4) * 4 + b % 4
        src = g_hbm.at[pl.ds(p * 64, 64)] if own else c
        return remote(src, c, sb_s.at[slot], sb_r.at[slot], {"dp": sib})

    def got_share(p, a, b):
        c = chunk(node(p, a, b, other), p)
        slot = p * 16 + (a % 4) * 4 + b % 4
        remote(c, c, sb_s.at[slot], sb_r.at[slot], {"dp": sib}).wait_recv()

    def chip_at(j):
        return chip ^ (j * 5 & 15)

    def peer(j):
        return me ^ (((j >> 1) * 5 & 15) * 2 + (j & 1))

    def columns(device):
        return pl.ds(pl.multiple_of(device * width, width), width)

    def x_copy(src_device, dst_device, slot):
        return remote(
            x_hbm.at[:, columns(dst_device)],
            xf.at[pl.ds(pl.multiple_of(src_device * rows, rows), rows)],
            x_s.at[slot], x_r.at[src_device], {"dp": dst_device},
        )

    def a_copy(src_device, dst_device, slot):
        return remote(
            at_hbm.at[:, columns(dst_device)],
            atf.at[pl.ds(pl.multiple_of(src_device * RANK, RANK), RANK)],
            a_s.at[slot], a_r.at[src_device], {"dp": dst_device},
        )

    own_g = pltpu.make_async_copy(g_hbm, g_all.at[pl.ds(pl.multiple_of(me * rows, rows), rows)], loc.at[0])
    own_x = pltpu.make_async_copy(
        x_hbm.at[:, columns(me)], xf.at[pl.ds(pl.multiple_of(me * rows, rows), rows)], loc.at[1]
    )
    own_a = pltpu.make_async_copy(
        at_hbm.at[:, columns(me)], atf.at[pl.ds(pl.multiple_of(me * RANK, RANK), RANK)], loc.at[2]
    )
    dirs = (1, -1)
    for d in dirs:
        for p in range(2):
            first(p, d).start()
    for d in dirs:
        for p in range(2):
            second(p, 0, d).start()
    own_g.start()
    for p in range(2):
        share(p, 0, 0, True).start()

    own_a.start()

    @pl.loop(1, 32)
    def _(j):
        a_copy(me, peer(j), j).start()

    blank = jnp.zeros((16, PAD, 128), BF16)
    upad[:, 0:PAD, :] = blank
    upad[:, PAD + WIN:, :] = blank

    for d in dirs:
        for p in range(2):
            got_first(p, d)
            fwd1(p, d).start()
            for e in dirs:
                second(p, (-d) % 4, e).start()
            share(p, -d, 0).start()
    for d in dirs:
        for p in range(2):
            got_second(p, 0, d)
            fwd2(p, 0, d).start()
            share(p, 0, -d).start()
    for p in range(2):
        for d in dirs:
            got_fwd1(p, d)
        for e in dirs:
            second(p, 2, e).start()
        share(p, 2, 0).start()
    for q in (3, 1):
        for d in dirs:
            for p in range(2):
                got_second(p, q, d)
                fwd2(p, q, d).start()
                share(p, q, -d).start()
    for p in range(2):
        for d in dirs:
            got_fwd2(p, 0, d)
        share(p, 0, 2).start()
    for d in dirs:
        for p in range(2):
            got_second(p, 2, d)
            fwd2(p, 2, d).start()
            share(p, 2, -d).start()
    for q in (3, 1, 2):
        for p in range(2):
            for d in dirs:
                got_fwd2(p, q, d)
            share(p, q, 2).start()
    own_x.start()

    @pl.loop(1, 32)
    def _(j):
        x_copy(me, peer(j), j).start()

    own_g.wait()
    for p in range(2):
        for a in range(4):
            for b in range(4):
                got_share(p, a, b)

    s0 = start_of(me)
    lane = lax.broadcasted_iota(jnp.int32, (WIN, 128), 1)
    ut2 = jnp.concatenate([ut_ref[...], ut_ref[...]], axis=0)
    u_own = (mask[...] * dot(g_all[pl.ds(s0, WIN), :], ut2, NT)).astype(BF16)
    usib[0] = u_own
    to_sib = remote(usib.at[0], usib.at[1], us_s, us_r, {"dp": sib})
    to_sib.start()
    to_sib.wait_recv()
    upad[chip, PAD:PAD + WIN, :] = u_own + usib[1]

    def u_rows(c, part):
        return upad.at[c, pl.ds(pl.multiple_of(PAD + part * HALF, 16), HALF)]

    def u_copy(c, device):
        return remote(u_rows(c, core), u_rows(c, core), u_s.at[device >> 1], u_r.at[c], {"dp": device})

    def u_share(c, part):
        return remote(u_rows(c, part), u_rows(c, part), uf_s.at[c], uf_r.at[c], {"dp": sib})

    @pl.loop(1, 16)
    def _(j):
        u_copy(chip, chip_at(j) * 2 + core).start()

    own_a.wait()

    @pl.loop(1, 32)
    def _(j):
        a_copy(peer(j), me, j).wait_recv()

    own_x.wait()

    @pl.loop(1, 32)
    def _(j):
        x_copy(peer(j), me, j).wait_recv()

    @pl.loop(0, 16)
    def _(c):
        pair = atf[pl.ds(pl.multiple_of(c * 128, 128), 128), :]
        even = dot(xf[pl.ds(start_of(2 * c), WIN), :], pair, NT)
        odd = dot(xf[pl.ds(start_of(2 * c + 1), WIN), :], pair, NT)
        vp[c] = jnp.where(lane < RANK, even, odd)

    def half(part):
        return pl.ds(pl.multiple_of(part * HALF, 8), HALF)

    v_swap = remote(vp.at[:, half(other)], vsib, vs_s, vs_r, {"dp": sib})
    v_swap.start()

    @pl.loop(1, 16)
    def _(j):
        c = chip_at(j)
        u_copy(c, c * 2 + core).wait_recv()
        u_share(c, core).start()

    def v_copy(src_chip, dst_chip):
        return remote(vsib.at[dst_chip], vrecv.at[src_chip], v_s.at[dst_chip], v_r.at[src_chip], {"dp": dst_chip * 2 + core})

    v_swap.wait_recv()

    @pl.loop(1, 16)
    def _(j):
        c = chip_at(j)
        vsib[c] = vsib[c] + vp[c, half(core), :]
        v_copy(chip, c).start()

    @pl.loop(1, 16)
    def _(j):
        u_share(chip_at(j), other).wait_recv()

    pl.semaphore_wait(ready, 1)

    def p_copy(src_device, dst_device):
        return remote(
            p_stage.at[pl.ds(pl.multiple_of(dst_device * rows, rows), rows)],
            passed.at[:, columns(src_device)],
            p_s.at[dst_device], p_r.at[src_device], {"section": before, "dp": dst_device},
        )

    low = (lax.broadcasted_iota(jnp.int32, (2 * rows, 128), 1) < RANK).astype(F32).astype(BF16)
    high = (lax.broadcasted_iota(jnp.int32, (2 * rows, 128), 1) >= RANK).astype(F32).astype(BF16)

    def da_copy(src_device, dst_device):
        return remote(
            da_stage.at[pl.ds(pl.multiple_of(dst_device * RANK, RANK), RANK)],
            da_out.at[:, columns(src_device)],
            da_s.at[dst_device], da_r.at[src_device], {"dp": dst_device},
        )

    own_da = pltpu.make_async_copy(
        da_stage.at[pl.ds(pl.multiple_of(me * RANK, RANK), RANK)], da_out.at[:, columns(me)], loc.at[3]
    )

    @pl.loop(0, 16)
    def _(j):
        c = chip_at(j)

        @pl.when(z > 0)
        def _():
            base = pl.multiple_of(c * 2 * rows, 2 * rows)
            for k in range(16):
                even = spots[c, 2 * k] * 16
                odd = spots[c, 2 * k + 1] * 16
                uexp[:, k * 128:(k + 1) * 128] = (
                    upad[k, pl.ds(even, 2 * rows), :] * low + upad[k, pl.ds(odd, 2 * rows), :] * high
                )
            tile = dot(g_all[pl.ds(base, 2 * rows), :], w_ref[...], NT)
            tile = tile + 2.0 * dot(uexp[...], atf[...], NN)
            p_stage[pl.ds(base, 2 * rows), :] = tile.astype(BF16)
            p_copy(me, c * 2 + core).start()
            p_copy(me, c * 2 + other).start()

        u = upad[c, PAD:PAD + WIN, :]
        even = dot(u, xf[pl.ds(start_of(2 * c), WIN), :], TN)
        odd = dot(u, xf[pl.ds(start_of(2 * c + 1), WIN), :], TN)
        grad_row = lax.broadcasted_iota(jnp.int32, (128, width), 0)
        da_stage[pl.ds(pl.multiple_of(c * 128, 128), 128), :] = (
            2.0 * jnp.where(grad_row < RANK, even, odd)
        ).astype(BF16)

        @pl.when(j == 0)
        def _():
            own_da.start()

        @pl.when(j > 0)
        def _():
            da_copy(me, c * 2 + core).start()

        da_copy(me, c * 2 + other).start()

    @pl.when(z == last)
    def _():
        zero[...] = jnp.zeros_like(zero)

        @pl.loop(0, 32)
        def _(j):
            pltpu.make_async_copy(zero, passed.at[:, columns(j)], p_r.at[j]).start()

    total = vsib[chip] + vp[chip, half(core), :]

    def add(j, total):
        c = chip_at(j)
        v_copy(c, chip).wait_recv()
        return total + vrecv[c]

    vbf[half_bf(core), :] = lax.fori_loop(1, 16, add, total).astype(BF16)
    v_back = remote(vbf.at[half_bf(core)], vbf.at[half_bf(core)], vb_s, vb_r, {"dp": sib})
    v_back.start()
    remote(vbf.at[half_bf(other)], vbf.at[half_bf(other)], vb_s, vb_r, {"dp": sib}).wait_recv()
    v = (mask[...] * vbf[...].astype(F32)).astype(BF16)

    @pl.loop(0, 4)
    def _(i):
        part = pl.ds(pl.multiple_of(i * 512, 512), 512)
        dubuf[:, part] = (2.0 * dot(v, g_all[pl.ds(s0, WIN), part], TN)).astype(BF16)

    own_du = pltpu.make_async_copy(dubuf.at[pl.ds(pl.multiple_of(core * RANK, RANK), RANK)], du_out, loc.at[4])
    own_du.start()

    own_da.wait()
    own_du.wait()
    to_sib.wait_send()
    v_swap.wait_send()
    v_back.wait_send()
    for p in range(2):
        for d in dirs:
            first(p, d).wait_send()
            fwd1(p, d).wait_send()
            for q in range(4):
                second(p, q, d).wait_send()
                fwd2(p, q, d).wait_send()
        for a in range(4):
            for b in range(4):
                share(p, a, b).wait_send()

    @pl.loop(1, 32)
    def _(j):
        d = peer(j)
        a_copy(me, d, j).wait_send()
        x_copy(me, d, j).wait_send()
        da_copy(me, d).wait_send()
        da_copy(d, me).wait_recv()

    @pl.loop(1, 16)
    def _(j):
        c = chip_at(j)
        u_copy(chip, c * 2 + core).wait_send()
        u_share(c, core).wait_send()
        v_copy(chip, c).wait_send()

    @pl.when(z > 0)
    def _():
        @pl.loop(0, 32)
        def _(j):
            p_copy(me, j).wait_send()

    @pl.when(z < last)
    def _():
        @pl.loop(0, 32)
        def _(j):
            p_copy(j, me).wait_recv()

    @pl.when(z == last)
    def _():
        @pl.loop(0, 32)
        def _(j):
            pltpu.make_async_copy(zero, passed.at[:, columns(j)], p_r.at[j]).wait()


def half_bf(part):
    return pl.ds(pl.multiple_of(part * HALF, 16), HALF)


def local(output_gradient, saved_input, frozen_matrix, down_maps, up_maps, token_tenants, slot_lookup):
    tokens = token_tenants.shape[1]
    tenants = slot_lookup.shape[1]
    order = jnp.arange(tenants, dtype=jnp.int32)
    tenant_of = jnp.sum(jnp.where(slot_lookup[0][None, :] == order[:, None], order[None, :], 0), axis=1)
    row = token_tenants[0][None, :]
    start = jnp.sum((row < tenant_of[:, None]).astype(jnp.int32), axis=1)
    count = jnp.sum((row == tenant_of[:, None]).astype(jnp.int32), axis=1)
    meta = jnp.minimum(start // 16, (tokens - WIN) // 16)
    block = jnp.arange(16, dtype=jnp.int32) * (tokens // 256)
    spots = jnp.clip(PAD // 16 + block[:, None] - meta[None, :], 0, (PAD + WIN) // 16)
    me = lax.axis_index("dp")
    place = jnp.arange(WIN, dtype=jnp.int32)[:, None]
    offset = (start - meta * 16)[None, :]
    live = (place >= offset) & (place < offset + count[None, :]) & (order == me)[None, :]
    side = jnp.arange(128, dtype=jnp.int32)[None, :] >> 6
    mask = jnp.sum(live.astype(F32), axis=1, keepdims=True) * (side == (me & 1)).astype(F32)

    rows, kv = output_gradient.shape[1:]
    model = saved_input.shape[2]
    width = frozen_matrix.shape[1]
    hbm = pl.BlockSpec(memory_space=pl.ANY)
    vmem = pl.BlockSpec(memory_space=pltpu.VMEM)
    smem = pl.BlockSpec(memory_space=pltpu.SMEM)
    dma = pltpu.SemaphoreType.DMA
    passed, da, du = pl.pallas_call(
        kernel,
        out_shape=(
            jax.ShapeDtypeStruct((rows, model), BF16),
            jax.ShapeDtypeStruct((RANK, model), BF16),
            jax.ShapeDtypeStruct((RANK, kv), BF16),
        ),
        in_specs=[smem, smem, vmem, hbm, hbm, vmem, hbm, vmem],
        out_specs=(hbm, hbm, hbm),
        scratch_shapes=[
            pltpu.VMEM((tokens, kv), BF16),
            pltpu.VMEM((tokens, width), BF16),
            pltpu.VMEM((tenants * RANK, width), BF16),
            pltpu.VMEM((16, PAD + WIN + PAD, 128), BF16),
            pltpu.VMEM((2, WIN, 128), BF16),
            pltpu.VMEM((2 * rows, tenants * RANK), BF16),
            pltpu.VMEM((tokens, width), BF16),
            pltpu.VMEM((tenants * RANK, width), BF16),
            pltpu.VMEM((16, WIN, 128), F32),
            pltpu.VMEM((16, HALF, 128), F32),
            pltpu.VMEM((16, HALF, 128), F32),
            pltpu.VMEM((WIN, 128), BF16),
            pltpu.VMEM((128, kv), BF16),
            pltpu.VMEM((rows, width), BF16),
            pltpu.SemaphoreType.REGULAR,
            dma((5,)),
            dma((40,)), dma((40,)), dma((32,)), dma((32,)),
            dma((32,)), dma((32,)), dma((32,)), dma((32,)),
            dma, dma, dma((16,)), dma((16,)), dma((16,)), dma((16,)),
            dma((32,)), dma((32,)), dma((32,)), dma((32,)),
            dma, dma, dma((16,)), dma((16,)), dma, dma,
        ],
        compiler_params=pltpu.CompilerParams(collective_id=0, has_side_effects=True, vmem_limit_bytes=56 << 20),
    )(
        meta,
        spots,
        mask,
        output_gradient[0],
        saved_input[0],
        frozen_matrix[0],
        jnp.swapaxes(down_maps[0], 0, 1),
        jnp.swapaxes(up_maps[0], 0, 1),
    )
    return passed[None], jnp.swapaxes(da, 0, 1)[None], jnp.swapaxes(du, 0, 1)[None]


def solution(mesh):
    return jax.shard_map(
        local,
        mesh=mesh,
        in_specs=(
            P("section", "dp", None),
            P("section", "dp", None),
            P("section", "dp", None),
            P("section", None, "dp"),
            P("section", None, "dp"),
            P("section", None),
            P("section", None),
        ),
        out_specs=(P("section", "dp", None), P("section", None, "dp"), P("section", None, "dp")),
        check_vma=False,
    )
```

```python
import jax
import jax.numpy as jnp
from jax import lax
from jax.experimental import pallas as pl
from jax.experimental.pallas import tpu as pltpu
from jax.sharding import PartitionSpec as P

RANK = 64
WIN = 288
HALF = WIN // 2
PAD = 256
MESH = pl.DeviceIdType.MESH
NT = (((1,), (1,)), ((), ()))
NN = (((1,), (0,)), ((), ()))
TN = (((0,), (0,)), ((), ()))
F32 = jnp.float32
BF16 = jnp.bfloat16


def dot(a, b, dims):
    return lax.dot_general(a, b, dims, preferred_element_type=F32)


def remote(src, dst, send, recv, device):
    return pltpu.make_async_remote_copy(
        src_ref=src, dst_ref=dst, send_sem=send, recv_sem=recv, device_id=device, device_id_type=MESH
    )


def kernel(
    meta, spots, mask, g_hbm, x_hbm, w_ref, at_hbm, ut_ref, passed, da_out, du_out,
    g_all, xf, atf, upad, usib, uexp, p_stage, da_stage, vp, vsib, vrecv, vbf, dubuf, zero,
    ready, loc, ag_s, ag_r, sb_s, sb_r, x_s, x_r, a_s, a_r, us_s, us_r, u_s, u_r, uf_s, uf_r,
    p_s, p_r, da_s, da_r, vs_s, vs_r, v_s, v_r, vb_s, vb_r,
):
    z = lax.axis_index("section")
    me = lax.axis_index("dp")
    last = lax.axis_size("section") - 1
    core = me & 1
    other = core ^ 1
    chip = me >> 1
    sib = me ^ 1
    along_x = [((me >> 3) + d & 3) * 8 for d in range(4)]
    along_y = [(chip + d & 3) * 2 for d in range(4)]
    after = jnp.where(z == last, 0, z + 1)
    before = jnp.where(z == 0, last, z - 1)
    width = w_ref.shape[0]
    rows = g_hbm.shape[0]

    def start_of(slot):
        return meta[slot] * 16

    barrier = pltpu.get_barrier_semaphore()

    @pl.loop(1, 32)
    def _(j):
        pl.semaphore_signal(barrier, 1, device_id={"dp": me ^ j}, device_id_type=MESH)

    for section in (after, before):
        pl.semaphore_signal(barrier, 1, device_id={"section": section}, device_id_type=MESH)
    pl.semaphore_wait(barrier, 33)
    pl.semaphore_signal(ready, 1, device_id={"section": after}, device_id_type=MESH)

    def node(p, a, b, who=core):
        dx, dy = (b, a) if p == 0 else (a, b)
        return along_x[dx % 4] + along_y[dy % 4] + who

    def chunk(device, p, part=None):
        first = device * rows + p * 64
        if part is None:
            return g_all.at[pl.ds(pl.multiple_of(first, 64), 64)]
        return g_all.at[pl.ds(pl.multiple_of(first + part * 32, 32), 32)]

    def ag(src, dst, slot, device):
        return remote(src, dst, ag_s.at[slot], ag_r.at[slot], {"dp": device})

    def part_of(d):
        return 0 if d == 1 else 1

    def first(p, d):
        return ag(g_hbm.at[pl.ds(p * 64, 64)], chunk(me, p), p * 20 + part_of(d), node(p, d, 0))

    def got_first(p, d):
        c = chunk(node(p, -d, 0), p)
        ag(c, c, p * 20 + part_of(d), me).wait_recv()

    def fwd1(p, d):
        c = chunk(node(p, -d, 0), p, part_of(d))
        return ag(c, c, p * 20 + 2 + part_of(d), node(p, d, 0))

    def got_fwd1(p, d):
        c = chunk(node(p, 2, 0), p, part_of(d))
        ag(c, c, p * 20 + 2 + part_of(d), me).wait_recv()

    def second(p, q, d):
        c = chunk(node(p, q, 0), p)
        src = g_hbm.at[pl.ds(p * 64, 64)] if q == 0 else c
        return ag(src, c, p * 20 + 4 + q * 4 + part_of(d), node(p, 0, d))

    def got_second(p, q, d):
        c = chunk(node(p, q, -d), p)
        ag(c, c, p * 20 + 4 + q * 4 + part_of(d), me).wait_recv()

    def fwd2(p, q, d):
        c = chunk(node(p, q, -d), p, part_of(d))
        return ag(c, c, p * 20 + 4 + q * 4 + 2 + part_of(d), node(p, 0, d))

    def got_fwd2(p, q, d):
        c = chunk(node(p, q, 2), p, part_of(d))
        ag(c, c, p * 20 + 4 + q * 4 + 2 + part_of(d), me).wait_recv()

    def share(p, a, b, own=False):
        c = chunk(node(p, a, b), p)
        slot = p * 16 + (a % 4) * 4 + b % 4
        src = g_hbm.at[pl.ds(p * 64, 64)] if own else c
        return remote(src, c, sb_s.at[slot], sb_r.at[slot], {"dp": sib})

    def got_share(p, a, b):
        c = chunk(node(p, a, b, other), p)
        slot = p * 16 + (a % 4) * 4 + b % 4
        remote(c, c, sb_s.at[slot], sb_r.at[slot], {"dp": sib}).wait_recv()

    def chip_at(j):
        return chip ^ (j * 5 & 15)

    def peer(j):
        return me ^ ((j * 5 & 15) * 2 + (j >> 4))

    def columns(device):
        return pl.ds(pl.multiple_of(device * width, width), width)

    def x_copy(src_device, dst_device, slot):
        return remote(
            x_hbm.at[:, columns(dst_device)],
            xf.at[pl.ds(pl.multiple_of(src_device * rows, rows), rows)],
            x_s.at[slot], x_r.at[src_device], {"dp": dst_device},
        )

    def a_copy(src_device, dst_device, slot):
        return remote(
            at_hbm.at[:, columns(dst_device)],
            atf.at[pl.ds(pl.multiple_of(src_device * RANK, RANK), RANK)],
            a_s.at[slot], a_r.at[src_device], {"dp": dst_device},
        )

    own_g = pltpu.make_async_copy(g_hbm, g_all.at[pl.ds(pl.multiple_of(me * rows, rows), rows)], loc.at[0])
    own_x = pltpu.make_async_copy(
        x_hbm.at[:, columns(me)], xf.at[pl.ds(pl.multiple_of(me * rows, rows), rows)], loc.at[1]
    )
    own_a = pltpu.make_async_copy(
        at_hbm.at[:, columns(me)], atf.at[pl.ds(pl.multiple_of(me * RANK, RANK), RANK)], loc.at[2]
    )
    dirs = (1, -1)
    for d in dirs:
        for p in range(2):
            first(p, d).start()
    for d in dirs:
        for p in range(2):
            second(p, 0, d).start()
    own_g.start()
    for p in range(2):
        share(p, 0, 0, True).start()

    own_a.start()

    blank = jnp.zeros((16, PAD, 128), BF16)
    upad[:, 0:PAD, :] = blank
    upad[:, PAD + WIN:, :] = blank

    for d in dirs:
        for p in range(2):
            got_first(p, d)
            fwd1(p, d).start()
            for e in dirs:
                second(p, (-d) % 4, e).start()
            share(p, -d, 0).start()
    for d in dirs:
        for p in range(2):
            got_second(p, 0, d)
            fwd2(p, 0, d).start()
            share(p, 0, -d).start()
    for p in range(2):
        for d in dirs:
            got_fwd1(p, d)
        for e in dirs:
            second(p, 2, e).start()
        share(p, 2, 0).start()
    for q in (3, 1):
        for d in dirs:
            for p in range(2):
                got_second(p, q, d)
                fwd2(p, q, d).start()
                share(p, q, -d).start()
    for p in range(2):
        for d in dirs:
            got_fwd2(p, 0, d)
        share(p, 0, 2).start()
    for d in dirs:
        for p in range(2):
            got_second(p, 2, d)
            fwd2(p, 2, d).start()
            share(p, 2, -d).start()
    for q in (3, 1, 2):
        for p in range(2):
            for d in dirs:
                got_fwd2(p, q, d)
            share(p, q, 2).start()
    @pl.loop(1, 32)
    def _(j):
        a_copy(me, peer(j), j).start()

    own_x.start()

    @pl.loop(1, 32)
    def _(j):
        x_copy(me, peer(j), j).start()

    own_g.wait()
    for p in range(2):
        for a in range(4):
            for b in range(4):
                got_share(p, a, b)

    s0 = start_of(me)
    lane = lax.broadcasted_iota(jnp.int32, (WIN, 128), 1)
    ut2 = jnp.concatenate([ut_ref[...], ut_ref[...]], axis=0)
    u_own = (mask[...] * dot(g_all[pl.ds(s0, WIN), :], ut2, NT)).astype(BF16)
    usib[0] = u_own
    to_sib = remote(usib.at[0], usib.at[1], us_s, us_r, {"dp": sib})
    to_sib.start()
    to_sib.wait_recv()
    upad[chip, PAD:PAD + WIN, :] = u_own + usib[1]

    def u_rows(c, part):
        return upad.at[c, pl.ds(pl.multiple_of(PAD + part * HALF, 16), HALF)]

    def u_copy(c, device):
        return remote(u_rows(c, core), u_rows(c, core), u_s.at[device >> 1], u_r.at[c], {"dp": device})

    def u_share(c, part):
        return remote(u_rows(c, part), u_rows(c, part), uf_s.at[c], uf_r.at[c], {"dp": sib})

    @pl.loop(1, 16)
    def _(j):
        u_copy(chip, chip_at(j) * 2 + core).start()

    own_a.wait()

    @pl.loop(1, 32)
    def _(j):
        a_copy(peer(j), me, j).wait_recv()

    own_x.wait()

    @pl.loop(1, 32)
    def _(j):
        x_copy(peer(j), me, j).wait_recv()

    @pl.loop(0, 16)
    def _(c):
        pair = atf[pl.ds(pl.multiple_of(c * 128, 128), 128), :]
        even = dot(xf[pl.ds(start_of(2 * c), WIN), :], pair, NT)
        odd = dot(xf[pl.ds(start_of(2 * c + 1), WIN), :], pair, NT)
        vp[c] = jnp.where(lane < RANK, even, odd)

    def half(part):
        return pl.ds(pl.multiple_of(part * HALF, 8), HALF)

    v_swap = remote(vp.at[:, half(other)], vsib, vs_s, vs_r, {"dp": sib})
    v_swap.start()

    @pl.loop(1, 16)
    def _(j):
        c = chip_at(j)
        u_copy(c, c * 2 + core).wait_recv()
        u_share(c, core).start()

    def v_copy(src_chip, dst_chip):
        return remote(vsib.at[dst_chip], vrecv.at[src_chip], v_s.at[dst_chip], v_r.at[src_chip], {"dp": dst_chip * 2 + core})

    v_swap.wait_recv()

    @pl.loop(1, 16)
    def _(j):
        c = chip_at(j)
        vsib[c] = vsib[c] + vp[c, half(core), :]
        v_copy(chip, c).start()

    @pl.loop(1, 16)
    def _(j):
        u_share(chip_at(j), other).wait_recv()

    pl.semaphore_wait(ready, 1)

    def p_copy(src_device, dst_device):
        return remote(
            p_stage.at[pl.ds(pl.multiple_of(dst_device * rows, rows), rows)],
            passed.at[:, columns(src_device)],
            p_s.at[dst_device], p_r.at[src_device], {"section": before, "dp": dst_device},
        )

    low = (lax.broadcasted_iota(jnp.int32, (2 * rows, 128), 1) < RANK).astype(F32).astype(BF16)
    high = (lax.broadcasted_iota(jnp.int32, (2 * rows, 128), 1) >= RANK).astype(F32).astype(BF16)

    def da_copy(src_device, dst_device):
        return remote(
            da_stage.at[pl.ds(pl.multiple_of(dst_device * RANK, RANK), RANK)],
            da_out.at[:, columns(src_device)],
            da_s.at[dst_device], da_r.at[src_device], {"dp": dst_device},
        )

    own_da = pltpu.make_async_copy(
        da_stage.at[pl.ds(pl.multiple_of(me * RANK, RANK), RANK)], da_out.at[:, columns(me)], loc.at[3]
    )

    @pl.loop(0, 16)
    def _(j):
        c = chip_at(j)

        @pl.when(z > 0)
        def _():
            base = pl.multiple_of(c * 2 * rows, 2 * rows)
            for k in range(16):
                even = spots[c, 2 * k] * 16
                odd = spots[c, 2 * k + 1] * 16
                uexp[:, k * 128:(k + 1) * 128] = (
                    upad[k, pl.ds(even, 2 * rows), :] * low + upad[k, pl.ds(odd, 2 * rows), :] * high
                )
            tile = dot(g_all[pl.ds(base, 2 * rows), :], w_ref[...], NT)
            tile = tile + 2.0 * dot(uexp[...], atf[...], NN)
            p_stage[pl.ds(base, 2 * rows), :] = tile.astype(BF16)
            p_copy(me, c * 2 + core).start()
            p_copy(me, c * 2 + other).start()

    @pl.loop(0, 16)
    def _(j):
        c = chip_at(j)
        u = upad[c, PAD:PAD + WIN, :]
        even = dot(u, xf[pl.ds(start_of(2 * c), WIN), :], TN)
        odd = dot(u, xf[pl.ds(start_of(2 * c + 1), WIN), :], TN)
        grad_row = lax.broadcasted_iota(jnp.int32, (128, width), 0)
        da_stage[pl.ds(pl.multiple_of(c * 128, 128), 128), :] = (
            2.0 * jnp.where(grad_row < RANK, even, odd)
        ).astype(BF16)

        @pl.when(j == 0)
        def _():
            own_da.start()

        @pl.when(j > 0)
        def _():
            da_copy(me, c * 2 + core).start()

        da_copy(me, c * 2 + other).start()

    @pl.when(z == last)
    def _():
        zero[...] = jnp.zeros_like(zero)

        @pl.loop(0, 32)
        def _(j):
            pltpu.make_async_copy(zero, passed.at[:, columns(j)], p_r.at[j]).start()

    total = vsib[chip] + vp[chip, half(core), :]

    def add(j, total):
        c = chip_at(j)
        v_copy(c, chip).wait_recv()
        return total + vrecv[c]

    vbf[half_bf(core), :] = lax.fori_loop(1, 16, add, total).astype(BF16)
    v_back = remote(vbf.at[half_bf(core)], vbf.at[half_bf(core)], vb_s, vb_r, {"dp": sib})
    v_back.start()
    remote(vbf.at[half_bf(other)], vbf.at[half_bf(other)], vb_s, vb_r, {"dp": sib}).wait_recv()
    v = (mask[...] * vbf[...].astype(F32)).astype(BF16)

    @pl.loop(0, 4)
    def _(i):
        part = pl.ds(pl.multiple_of(i * 512, 512), 512)
        dubuf[:, part] = (2.0 * dot(v, g_all[pl.ds(s0, WIN), part], TN)).astype(BF16)

    own_du = pltpu.make_async_copy(dubuf.at[pl.ds(pl.multiple_of(core * RANK, RANK), RANK)], du_out, loc.at[4])
    own_du.start()

    own_da.wait()
    own_du.wait()
    to_sib.wait_send()
    v_swap.wait_send()
    v_back.wait_send()
    for p in range(2):
        for d in dirs:
            first(p, d).wait_send()
            fwd1(p, d).wait_send()
            for q in range(4):
                second(p, q, d).wait_send()
                fwd2(p, q, d).wait_send()
        for a in range(4):
            for b in range(4):
                share(p, a, b).wait_send()

    @pl.loop(1, 32)
    def _(j):
        d = peer(j)
        a_copy(me, d, j).wait_send()
        x_copy(me, d, j).wait_send()
        da_copy(me, d).wait_send()
        da_copy(d, me).wait_recv()

    @pl.loop(1, 16)
    def _(j):
        c = chip_at(j)
        u_copy(chip, c * 2 + core).wait_send()
        u_share(c, core).wait_send()
        v_copy(chip, c).wait_send()

    @pl.when(z > 0)
    def _():
        @pl.loop(0, 32)
        def _(j):
            p_copy(me, j).wait_send()

    @pl.when(z < last)
    def _():
        @pl.loop(0, 32)
        def _(j):
            p_copy(j, me).wait_recv()

    @pl.when(z == last)
    def _():
        @pl.loop(0, 32)
        def _(j):
            pltpu.make_async_copy(zero, passed.at[:, columns(j)], p_r.at[j]).wait()


def half_bf(part):
    return pl.ds(pl.multiple_of(part * HALF, 16), HALF)


def local(output_gradient, saved_input, frozen_matrix, down_maps, up_maps, token_tenants, slot_lookup):
    tokens = token_tenants.shape[1]
    tenants = slot_lookup.shape[1]
    order = jnp.arange(tenants, dtype=jnp.int32)
    tenant_of = jnp.sum(jnp.where(slot_lookup[0][None, :] == order[:, None], order[None, :], 0), axis=1)
    row = token_tenants[0][None, :]
    start = jnp.sum((row < tenant_of[:, None]).astype(jnp.int32), axis=1)
    count = jnp.sum((row == tenant_of[:, None]).astype(jnp.int32), axis=1)
    meta = jnp.minimum(start // 16, (tokens - WIN) // 16)
    block = jnp.arange(16, dtype=jnp.int32) * (tokens // 256)
    spots = jnp.clip(PAD // 16 + block[:, None] - meta[None, :], 0, (PAD + WIN) // 16)
    me = lax.axis_index("dp")
    place = jnp.arange(WIN, dtype=jnp.int32)[:, None]
    offset = (start - meta * 16)[None, :]
    live = (place >= offset) & (place < offset + count[None, :]) & (order == me)[None, :]
    side = jnp.arange(128, dtype=jnp.int32)[None, :] >> 6
    mask = jnp.sum(live.astype(F32), axis=1, keepdims=True) * (side == (me & 1)).astype(F32)

    rows, kv = output_gradient.shape[1:]
    model = saved_input.shape[2]
    width = frozen_matrix.shape[1]
    hbm = pl.BlockSpec(memory_space=pl.ANY)
    vmem = pl.BlockSpec(memory_space=pltpu.VMEM)
    smem = pl.BlockSpec(memory_space=pltpu.SMEM)
    dma = pltpu.SemaphoreType.DMA
    passed, da, du = pl.pallas_call(
        kernel,
        out_shape=(
            jax.ShapeDtypeStruct((rows, model), BF16),
            jax.ShapeDtypeStruct((RANK, model), BF16),
            jax.ShapeDtypeStruct((RANK, kv), BF16),
        ),
        in_specs=[smem, smem, vmem, hbm, hbm, vmem, hbm, vmem],
        out_specs=(hbm, hbm, hbm),
        scratch_shapes=[
            pltpu.VMEM((tokens, kv), BF16),
            pltpu.VMEM((tokens, width), BF16),
            pltpu.VMEM((tenants * RANK, width), BF16),
            pltpu.VMEM((16, PAD + WIN + PAD, 128), BF16),
            pltpu.VMEM((2, WIN, 128), BF16),
            pltpu.VMEM((2 * rows, tenants * RANK), BF16),
            pltpu.VMEM((tokens, width), BF16),
            pltpu.VMEM((tenants * RANK, width), BF16),
            pltpu.VMEM((16, WIN, 128), F32),
            pltpu.VMEM((16, HALF, 128), F32),
            pltpu.VMEM((16, HALF, 128), F32),
            pltpu.VMEM((WIN, 128), BF16),
            pltpu.VMEM((128, kv), BF16),
            pltpu.VMEM((rows, width), BF16),
            pltpu.SemaphoreType.REGULAR,
            dma((5,)),
            dma((40,)), dma((40,)), dma((32,)), dma((32,)),
            dma((32,)), dma((32,)), dma((32,)), dma((32,)),
            dma, dma, dma((16,)), dma((16,)), dma((16,)), dma((16,)),
            dma((32,)), dma((32,)), dma((32,)), dma((32,)),
            dma, dma, dma((16,)), dma((16,)), dma, dma,
        ],
        compiler_params=pltpu.CompilerParams(collective_id=0, has_side_effects=True, vmem_limit_bytes=56 << 20),
    )(
        meta,
        spots,
        mask,
        output_gradient[0],
        saved_input[0],
        frozen_matrix[0],
        jnp.swapaxes(down_maps[0], 0, 1),
        jnp.swapaxes(up_maps[0], 0, 1),
    )
    return passed[None], jnp.swapaxes(da, 0, 1)[None], jnp.swapaxes(du, 0, 1)[None]


def solution(mesh):
    return jax.shard_map(
        local,
        mesh=mesh,
        in_specs=(
            P("section", "dp", None),
            P("section", "dp", None),
            P("section", "dp", None),
            P("section", None, "dp"),
            P("section", None, "dp"),
            P("section", None),
            P("section", None),
        ),
        out_specs=(P("section", "dp", None), P("section", None, "dp"), P("section", None, "dp")),
        check_vma=False,
    )
```
